256 devices in a mesh: row: 16 (over z, y_lo), col: 8 (over x, y_hi), rep: 2 (over core).
Axes of the slice: x: 4, y: 4 (y_hi: 2, y_lo: 2; y = y_hi * 2 + y_lo), z: 8, core: 2. Of those that a mesh axis runs over, the one named last changes fastest.
Arguments:
- activations: bfloat16 [2048, 7168], P(('col', 'rep'), 'row'), may hold values from -6 to 6
- out_grad: bfloat16 [2048, 7168], P(('col', 'rep'), 'row'), may hold values from -1.5 to 1.5
- up_codes: int32 [7168, 18432], P('row', 'col'), may hold values from 0 to 253
- up_scales: int32 [224, 18432], P('row', 'col'), may hold values from -15 to -12
- down_codes: int32 [18432, 7168], P('col', 'row'), may hold values from 0 to 253
- down_scales: int32 [576, 7168], P('col', 'row'), may hold values from -15 to -12
Outputs:
- layer_out: bfloat16 [2048, 7168], P(('col', 'rep'), 'row')
- in_grad: bfloat16 [2048, 7168], P(('col', 'rep'), 'row')
- up_grad: bfloat16 [7168, 18432], P('row', 'col')
- down_grad: bfloat16 [18432, 7168], P('col', 'row')
The draws below stay inside these ranges and needn't reach their ends.
All inputs are finite; a program needn't handle non-finite values.
Results may differ from the reference program's by a relative error of at most 0.025.
Values may be sent and summed in bfloat16 or wider, within the bound.
A program may use at most 128 MiB of HBM per device.

```python
import jax
import jax.numpy as jnp
from jax import lax

D = 7168
FF = 18432
BLOCK = 32
TOK = 1024
TOKENS = 2048
N_ROW = 16
N_COL = 8
N_REP = 2


def plant(array, own_key, least, high):
    longest = array.shape.index(max(array.shape))
    spots = []
    for shift in (0, 1):
        where = [jax.random.randint(jax.random.fold_in(own_key, axis), (), 0, length) for axis, length in enumerate(array.shape)]
        where[longest] = (where[longest] + shift) % array.shape[longest]
        spots.append(tuple(where))
    return array.at[spots[0]].set(least).at[spots[1]].set(high)


def level_of(stream_key, extent, shards, smallest, largest):
    level, own = 1.0, jax.random.fold_in(stream_key, 6)
    for axis_at, blocks in shards:
        steps = jnp.exp(jax.random.uniform(jax.random.fold_in(own, axis_at), (blocks,), jnp.float32, smallest / len(shards), largest / len(shards)))
        level = level * jnp.repeat(steps, extent[axis_at] // blocks).reshape([-1 if axis == axis_at else 1 for axis in range(len(extent))])
    return level


def noise(stream_key, dims, scale, limit, shards=(), kind=jnp.bfloat16):
    entries = jax.random.normal(stream_key, dims, jnp.float32) * scale
    if len(shards) > 0:
        entries = level_of(stream_key, dims, shards, -0.22, 0.18) * entries
    return jnp.clip(entries, min=-limit, max=limit).astype(kind)


def setup_inputs(seed: int = 0) -> dict:
    keys = jax.random.split(jax.random.key(seed), 7)
    return {
        "activations": noise(keys[0], (TOKENS, D), 1.0, 6.0, ((0, 16), (1, 16))),
        "out_grad": noise(keys[1], (TOKENS, D), 0.25, 1.5, ((0, 16), (1, 16))),
        "up_codes": plant(jax.random.randint(keys[2], (D, FF), 0, 254), jax.random.fold_in(keys[2], 1), 0, 253).astype(jnp.int32),
        "up_scales": plant(jax.random.randint(keys[3], (D // BLOCK, FF), -15, -11), jax.random.fold_in(keys[3], 1), -15, (-11) - 1).astype(jnp.int32),
        "down_codes": plant(jax.random.randint(keys[4], (FF, D), 0, 254), jax.random.fold_in(keys[4], 1), 0, 253).astype(jnp.int32),
        "down_scales": plant(jax.random.randint(keys[5], (FF // BLOCK, D), -15, -11), jax.random.fold_in(keys[5], 1), -15, (-11) - 1).astype(jnp.int32),
    }


def decode(code_words, scale_exps, block_size):
    sign_bit = code_words // 127
    magnitude = code_words % 127
    exponent = magnitude // 8
    mantissa = magnitude % 8
    normal = exponent > 0
    rows_count = scale_exps.shape[0]
    cols_count = scale_exps.shape[1]
    scale_grid = jnp.broadcast_to(scale_exps[:, None, :], (rows_count, block_size, cols_count)).reshape(code_words.shape)
    shift_count = -(jnp.where(normal, exponent - 10, -9) + scale_grid)
    factor = jnp.ones(code_words.shape, jnp.float32)
    halvings = (0.5, 0.25, 0.0625, 0.00390625, 1.52587890625e-05)
    for position in range(5):
        chosen = (shift_count // (2 ** position)) % 2 == 1
        factor = factor * jnp.where(chosen, jnp.float32(halvings[position]), jnp.float32(1.0))
    mant_value = jnp.where(normal, mantissa + 8, mantissa).astype(jnp.float32)
    signed = (1 - 2 * sign_bit).astype(jnp.float32)
    return (mant_value * factor * signed).astype(jnp.bfloat16)


def gelu_parts(pre_total):
    cdf_value = 0.5 * (1.0 + jax.scipy.special.erf(pre_total * 0.7071067811865476))
    density = jnp.exp(-0.5 * pre_total * pre_total) * 0.3989422804014327
    return pre_total * cdf_value, cdf_value + pre_total * density


def rounded_f32(value):
    low = lax.optimization_barrier(value.astype(jnp.bfloat16))
    return low.astype(jnp.float32)


def block_sum(left, right, blocks, right_rows):
    width = left.shape[1] // blocks
    total = jnp.zeros((left.shape[0], right.shape[1] if right_rows else right.shape[0]), jnp.float32)
    for index in range(blocks):
        piece = left[:, index * width:(index + 1) * width]
        if right_rows:
            other = right[index * width:(index + 1) * width, :]
            term = jnp.dot(piece, other, preferred_element_type=jnp.float32)
        else:
            other = right[:, index * width:(index + 1) * width]
            term = lax.dot_general(piece, other, (((1,), (1,)), ((), ())), preferred_element_type=jnp.float32)
        total = total + rounded_f32(term)
    return total


def split_replicas(whole, shard_rows):
    cols_count = whole.shape[1]
    return whole.reshape(N_COL, N_REP, shard_rows, cols_count).transpose(1, 0, 2, 3).reshape(N_REP, N_COL * shard_rows, cols_count)


def join_replicas(parts, shard_rows):
    cols_count = parts.shape[2]
    return parts.reshape(N_REP, N_COL, shard_rows, cols_count).transpose(1, 0, 2, 3).reshape(N_REP * N_COL * shard_rows, cols_count)


def reference(activations, out_grad, up_codes, up_scales, down_codes, down_scales):
    up_weight = decode(up_codes, up_scales, BLOCK)
    down_weight = decode(down_codes, down_scales, BLOCK)
    shard_rows = TOK // N_COL
    acts_rep = split_replicas(activations, shard_rows)
    grads_rep = split_replicas(out_grad, shard_rows)
    outs_list = []
    ingrad_list = []
    down_total = jnp.zeros((FF, D), jnp.float32)
    up_total = jnp.zeros((D, FF), jnp.float32)
    first_dims = (((0,), (0,)), ((), ()))
    for replica in range(N_REP):
        acts_now = acts_rep[replica]
        grads_now = grads_rep[replica]
        pre_total = block_sum(acts_now, up_weight, N_ROW, True)
        back_total = block_sum(grads_now, down_weight, N_ROW, False)
        activated, gelu_slope = gelu_parts(pre_total)
        gelu_out = activated.astype(jnp.bfloat16)
        hidden_grad = (back_total * gelu_slope).astype(jnp.bfloat16)
        outs_list.append(block_sum(gelu_out, down_weight, N_COL, True).astype(jnp.bfloat16))
        ingrad_list.append(block_sum(hidden_grad, up_weight, N_COL, False).astype(jnp.bfloat16))
        down_term = lax.dot_general(gelu_out, grads_now, first_dims, preferred_element_type=jnp.float32)
        down_total = down_total + rounded_f32(down_term)
        up_term = lax.dot_general(acts_now, hidden_grad, first_dims, preferred_element_type=jnp.float32)
        up_total = up_total + rounded_f32(up_term)
    layer_out = join_replicas(jnp.stack(outs_list), shard_rows)
    in_grad = join_replicas(jnp.stack(ingrad_list), shard_rows)
    return (layer_out, in_grad, up_total.astype(jnp.bfloat16), down_total.astype(jnp.bfloat16))
```

```python
import functools

import jax
import jax.numpy as jnp
from jax import lax
from jax.experimental import pallas as pl
from jax.experimental.pallas import tpu as pltpu
from jax.sharding import PartitionSpec as P

MESH = pl.DeviceIdType.MESH
BLOCK = 32
NCH = 3
F32 = jnp.float32
BF16 = jnp.bfloat16
GATHER = (("ya", "yb", "xa", "xb"), ("ya", "xb", "xa", "yb"))
HALVE = (("xa", "xb", "ya", "yb"), ("yb", "ya", "xb", "xa"))


def decode(codes, scales):
    rows, cols = codes.shape
    codes = codes.reshape(rows // BLOCK, BLOCK, cols)
    negative = codes >= 127
    size = jnp.where(negative, codes - 127, codes)
    mant = (size & 7) | (jnp.minimum(size, 8) & 8)
    whole = mant << (jnp.maximum(size >> 3, 1) - 1)
    unit = (1 << (scales + 15)).astype(F32) * (2.0**-24)
    value = whole.astype(F32) * unit[:, None, :]
    return jnp.where(negative, -value, value).astype(BF16).reshape(rows, cols)


def nn(a, b):
    return jnp.dot(a, b, preferred_element_type=F32)


def nt(a, b):
    return lax.dot_general(a, b, (((1,), (1,)), ((), ())), preferred_element_type=F32)


def tn(a, b):
    return lax.dot_general(a, b, (((0,), (0,)), ((), ())), preferred_element_type=F32)


def kernel(
    nz, x_in, dy_in, wu_in, wd_in,
    lo, ig, up_out, down_out,
    tok_v, wu_v, wd_v, rs_rcv, rs_snd, pre_v, ag, ug, dg, acc, obuf, rbuf,
    gs_u, gs_d, gr_u, gr_d, nb_u, nb_d,
    loc_sem, g_snd, g_rcv, w_snd, w_rcv, rs_ss, rs_rs, ag_ss, ag_rs, p_ss, p_rs, t_snd, t_rcv, t_loc,
):
    t, feats = x_in.shape[1], x_in.shape[2]
    hid = wu_in.shape[1] // 2
    ch = hid // NCH
    fh, chh = feats // 2, ch // 2
    row, col, rep = lax.axis_index("row"), lax.axis_index("col"), lax.axis_index("rep")
    z, yl = row // 2, row % 2
    xx, yh = col // 2, col % 2
    oh, orep = 1 - yl, 1 - rep

    def place(dims):
        a, b = int("ya" in dims), int("yb" in dims)
        nyl, nyh = (yl + a + b) % 2, (yh + b) % 2
        if "xa" in dims and "xb" in dims:
            nx = (xx + 2) % 4
        elif "xa" in dims:
            nx = xx + 1 - 2 * (xx % 2)
        elif "xb" in dims:
            nx = 3 - xx
        else:
            nx = xx
        return nyl, 2 * nx + nyh

    def plane(dim):
        nyl, ncol = place((dim,))
        return (2 * z + nyl, ncol, rep)

    zp = (2 * ((z + 1) % nz) + yl, col, rep)
    zm = (2 * ((z + nz - 1) % nz) + yl, col, rep)
    twin = (row, col, orep)
    ring = (zp, zm)

    def remote(src, dst, ssem, rsem, dev):
        return pltpu.make_async_remote_copy(
            src_ref=src, dst_ref=dst, send_sem=ssem, recv_sem=rsem, device_id=dev, device_id_type=MESH
        )

    barrier = pltpu.get_barrier_semaphore()
    for dev in (zp, zm, twin, plane("ya"), plane("yb"), plane("xa"), plane("xb")):
        pl.semaphore_signal(barrier, inc=1, device_id=dev, device_id_type=MESH)
    pl.semaphore_wait(barrier, 7)

    def lanes(half, j):
        return pl.ds(pl.multiple_of(half * hid + j * ch, 128), ch)

    def rows(start, size):
        return pl.ds(pl.multiple_of(start, 16), size)

    def w_first(m, j):
        if m == 0:
            src = wu_in.at[rows(rep * fh, fh), lanes(oh, j)]
            dst = wu_v.at[j, yl, rows(rep * fh, fh)]
        else:
            src = wd_in.at[rows(oh * hid + j * ch + rep * chh, chh)]
            dst = wd_v.at[j, yl, rows(rep * chh, chh)]
        return remote(src, dst, w_snd.at[0, m, j], w_rcv.at[0, m, j], plane("ya"))

    def w_second(m, j):
        ref = (wu_v.at[j, oh, rows(rep * fh, fh)], wd_v.at[j, oh, rows(rep * chh, chh)])[m]
        return remote(ref, ref, w_snd.at[1, m, j], w_rcv.at[1, m, j], twin)

    def w_local(m, j):
        if m == 0:
            return pltpu.make_async_copy(wu_in.at[:, lanes(yl, j)], wu_v.at[j, yl], loc_sem.at[m, j])
        return pltpu.make_async_copy(wd_in.at[rows(yl * hid + j * ch, ch)], wd_v.at[j, yl], loc_sem.at[m, j])

    tok_in = (x_in, dy_in)

    def spot(m, code):
        dims = tuple(GATHER[m][k] for k in range(4) if code >> k & 1)
        nyl, ncol = place(dims)
        return tok_v.at[m, nyl, :, rows(ncol * t, t)]

    def g_copy(m, code, step):
        src = tok_in[m] if code == 0 else spot(m, code)
        new = code + 2**step
        return remote(src, spot(m, code), g_snd.at[m, new], g_rcv.at[m, new], plane(GATHER[m][step]))

    def g_wait(m, code):
        here = spot(m, code)
        remote(here, here, g_snd.at[m, code], g_rcv.at[m, code], twin).wait_recv()

    for step in range(1, 4):
        for m in range(2):
            g_copy(m, 0, step).start()
    for m in range(2):
        g_copy(m, 0, 0).start()
    for j in range(NCH):
        for m in range(2):
            w_first(m, j).start()
    tok_local = [pltpu.make_async_copy(tok_in[m], spot(m, 0), loc_sem.at[2, m]) for m in range(2)]
    for m in range(2):
        tok_local[m].start()
        for j in range(NCH):
            w_local(m, j).start()

    ug[...] = jnp.zeros_like(ug)
    dg[...] = jnp.zeros_like(dg)
    for m in range(2):
        for j in range(NCH):
            rs_rcv[m, j, 0] = jnp.zeros(rs_rcv.shape[3:], BF16)

    for code in range(1, 16):
        for m in range(2):
            g_wait(m, code)
            for step in range(4):
                if 2**step > code:
                    g_copy(m, code, step).start()
    for m in range(2):
        tok_local[m].wait()

    def rs_copy(m, j, s):
        return remote(rs_snd.at[m, j, s], rs_rcv.at[m, j, s + 1], rs_ss.at[m, j, s], rs_rs.at[m, j, s + 1], ring[m])

    def rs_wait(m, j, s):
        here = rs_rcv.at[m, j, s]
        remote(here, here, rs_ss.at[m, j, s], rs_rs.at[m, j, s], twin).wait_recv()

    def term(m, j, b):
        if m == 0:
            return nn(tok_v[0, 0, b], wu_v[j, 0]) + nn(tok_v[0, 1, b], wu_v[j, 1])
        return nt(tok_v[1, 0, b], wd_v[j, 0]) + nt(tok_v[1, 1, b], wd_v[j, 1])

    def rs_step(i, carry):
        s, j = i // NCH, i % NCH

        @pl.when(s == 0)
        def _():
            for m in range(2):
                w_first(m, j).wait_recv()
                w_second(m, j).start()
            for m in range(2):
                w_local(m, j).wait()
                w_second(m, j).wait_recv()

        for m in range(2):
            b = (z + nz - 1 - s) % nz if m == 0 else (z + 1 + s) % nz
            part = term(m, j, b)

            @pl.when(s > 0)
            def _():
                rs_wait(m, j, s)

            rs_snd[m, j, s] = (part + rs_rcv[m, j, s].astype(F32)).astype(BF16)
            rs_copy(m, j, s).start()
        return carry

    lax.fori_loop(0, NCH * (nz - 1), rs_step, 0)

    def ag_copy(m, j, s):
        return remote(ag.at[m, j, s], ag.at[m, j, s + 1], ag_ss.at[m, j, s], ag_rs.at[m, j, s + 1], ring[m])

    def ag_wait(m, j, s):
        here = ag.at[m, j, s]
        remote(here, here, ag_ss.at[m, j, s], ag_rs.at[m, j, s], twin).wait_recv()

    def gelu_step(j, carry):
        for m in range(2):
            pre_v[m] = term(m, j, z)
        for m in range(2):
            rs_wait(m, j, nz - 1)
        pre = pre_v[0] + rs_rcv[0, j, nz - 1].astype(F32)
        back = pre_v[1] + rs_rcv[1, j, nz - 1].astype(F32)
        cdf = 0.5 * (1.0 + lax.erf(pre * 0.7071067811865476))
        density = jnp.exp(-0.5 * pre * pre) * 0.3989422804014327
        ag[0, j, 0] = (pre * cdf).astype(BF16)
        ag[1, j, 0] = (back * (cdf + pre * density)).astype(BF16)
        for m in range(2):
            ag_copy(m, j, 0).start()
        return carry

    lax.fori_loop(0, NCH, gelu_step, 0)

    widths = (8, 4, 2, 1)
    offs = (0, 8, 12, 14)

    def p_copy(m, k, s):
        w = widths[k]
        return remote(
            obuf.at[m, s, pl.ds(w, w)], rbuf.at[m, s, pl.ds(offs[k], w)],
            p_ss.at[m, k, s], p_rs.at[m, k, s], plane(HALVE[m][k]),
        )

    def p_first(m, s):
        for code in range(16):
            dims = tuple(HALVE[m][k] for k in range(4) if code >> (3 - k) & 1)
            nyl, ncol = place(dims)
            obuf[m, s, code] = acc[m, nyl, rows(ncol * t, t)].astype(BF16)
        p_copy(m, 0, s).start()

    def p_next(m, k, s):
        w = widths[k]
        p_copy(m, k, s).wait_recv()
        both = obuf[m, s, 0:w].astype(F32) + rbuf[m, s, offs[k] : offs[k] + w].astype(F32)
        if k < 3:
            obuf[m, s, 0:w] = both.astype(BF16)
            p_copy(m, k + 1, s).start()
        else:
            b = (z + nz - s) % nz if m == 0 else (z + s) % nz
            (lo, ig)[m][rows(b * t, t)] = both[0].astype(BF16)

    def p_step(s):
        for k in range(3, -1, -1):
            q = s - 1 - k

            @pl.when(jnp.logical_and(q >= 0, q < nz))
            def _():
                for m in range(2):
                    p_next(m, k, q)

    def ag_step(i, carry):
        s, j = i // NCH, i % NCH
        for m in range(2):

            @pl.when(s > 0)
            def _():
                ag_wait(m, j, s)

            @pl.when(jnp.logical_and(s > 0, s < nz - 1))
            def _():
                ag_copy(m, j, s).start()

        @pl.when(j == 0)
        def _():
            acc[...] = jnp.zeros_like(acc)

        for y in range(2):
            acc[0, y] += nn(ag[0, j, s], wd_v[j, y])
            acc[1, y] += nt(ag[1, j, s], wu_v[j, y])

        @pl.when(s % 2 == 1)
        def _():
            a_pair = jnp.concatenate([ag[0, j, s - 1], ag[0, j, s]], axis=0)
            h_pair = jnp.concatenate([ag[1, j, s - 1], ag[1, j, s]], axis=0)
            a0, a1 = (z + nz - s + 1) % nz, (z + nz - s) % nz
            h0, h1 = (z + s - 1) % nz, (z + s) % nz
            for y in range(2):
                dg[j, y] += tn(a_pair, jnp.concatenate([tok_v[1, y, a0], tok_v[1, y, a1]], axis=0))
                ug[j, y] += tn(jnp.concatenate([tok_v[0, y, h0], tok_v[0, y, h1]], axis=0), h_pair)

        @pl.when(j == NCH - 1)
        def _():
            for m in range(2):
                p_first(m, s)
            p_step(s)

        return carry

    lax.fori_loop(0, NCH * nz, ag_step, 0)

    def t_pair(m, j):
        src, dst = ((gs_u, gr_u), (gs_d, gr_d))[m]
        return remote(src.at[j], dst.at[j], t_snd.at[0, m, j], t_rcv.at[0, m, j], twin)

    def grad_half(m, j, y, who):
        if m == 0:
            return ug[j, y, rows(who * fh, fh)]
        return dg[j, y, rows(who * chh, chh)]

    def home(m, j, half, who):
        if m == 0:
            return up_out.at[rows(who * fh, fh), lanes(half, j)]
        return down_out.at[rows(half * hid + j * ch + who * chh, chh)]

    mine = (gr_u, gr_d)
    near = (nb_u, nb_d)

    def t_near(m, j):
        return remote(mine[m].at[j, oh], near[m].at[j], t_snd.at[1, m, j], t_rcv.at[1, m, j], plane("ya"))

    def t_own(m, j):
        return pltpu.make_async_copy(mine[m].at[j, yl], home(m, j, yl, rep), t_loc.at[0, m, j])

    def t_twin(m, j, who):
        return remote(mine[m].at[j, yl], home(m, j, yl, who), t_snd.at[2, m, j], t_rcv.at[2, m, j], twin)

    def t_far(m, j):
        return pltpu.make_async_copy(near[m].at[j], home(m, j, oh, rep), t_loc.at[1, m, j])

    def t_relay(m, j, who):
        return remote(near[m].at[j], home(m, j, oh, who), t_snd.at[3, m, j], t_rcv.at[3, m, j], twin)

    def t_a(j, carry):
        for m in range(2):
            for y in range(2):
                (gs_u, gs_d)[m][j, y] = grad_half(m, j, y, orep).astype(BF16)
            t_pair(m, j).start()
        return carry

    lax.fori_loop(0, NCH, t_a, 0)
    p_step(nz)

    def t_b(j, carry):
        for m in range(2):
            t_pair(m, j).wait_recv()
            for y in range(2):
                mine[m][j, y] = (grad_half(m, j, y, rep) + mine[m][j, y].astype(F32)).astype(BF16)
            t_near(m, j).start()
            t_own(m, j).start()
            t_twin(m, j, rep).start()
        return carry

    lax.fori_loop(0, NCH, t_b, 0)
    for s in range(nz + 1, nz + 4):
        p_step(s)

    def t_c(j, carry):
        for m in range(2):
            t_near(m, j).wait_recv()
            t_far(m, j).start()
            t_relay(m, j, rep).start()
        return carry

    lax.fori_loop(0, NCH, t_c, 0)

    def drain_t(j, carry):
        for m in range(2):
            t_own(m, j).wait()
            t_far(m, j).wait()
            t_twin(m, j, orep).wait_recv()
            t_relay(m, j, orep).wait_recv()
            t_pair(m, j).wait_send()
            t_near(m, j).wait_send()
            t_twin(m, j, rep).wait_send()
            t_relay(m, j, rep).wait_send()
            w_first(m, j).wait_send()
            w_second(m, j).wait_send()
        return carry

    lax.fori_loop(0, NCH, drain_t, 0)

    def drain_ring(i, carry):
        s, j = i // NCH, i % NCH
        for m in range(2):
            rs_copy(m, j, s).wait_send()
            ag_copy(m, j, s).wait_send()
        return carry

    lax.fori_loop(0, NCH * (nz - 1), drain_ring, 0)

    def drain_plane(s, carry):
        for m in range(2):
            for k in range(4):
                p_copy(m, k, s).wait_send()
        return carry

    lax.fori_loop(0, nz, drain_plane, 0)
    for m in range(2):
        for code in range(8):
            for step in range(4):
                if 2**step > code:
                    g_copy(m, code, step).wait_send()


def body(n_row, n_col, activations, out_grad, up_codes, up_scales, down_codes, down_scales):
    nz = n_row // 2
    tok, feats = activations.shape
    t = tok // nz
    hid2 = up_codes.shape[1]
    hid = hid2 // 2
    ch = hid // NCH
    span = n_col * t
    wu = decode(up_codes, up_scales)
    wd = decode(down_codes, down_scales)
    x = activations.reshape(nz, t, feats)
    dy = out_grad.reshape(nz, t, feats)
    hbm = pl.BlockSpec(memory_space=pl.ANY)
    vmem = pl.BlockSpec(memory_space=pltpu.VMEM)
    dma = pltpu.SemaphoreType.DMA
    return pl.pallas_call(
        functools.partial(kernel, nz),
        out_shape=(
            jax.ShapeDtypeStruct((tok, feats), BF16),
            jax.ShapeDtypeStruct((tok, feats), BF16),
            jax.ShapeDtypeStruct((feats, hid2), BF16),
            jax.ShapeDtypeStruct((hid2, feats), BF16),
        ),
        in_specs=[hbm] * 4,
        out_specs=(vmem, vmem, hbm, hbm),
        scratch_shapes=[
            pltpu.VMEM((2, 2, nz, span, feats), BF16),
            pltpu.VMEM((NCH, 2, feats, ch), BF16),
            pltpu.VMEM((NCH, 2, ch, feats), BF16),
            pltpu.VMEM((2, NCH, nz, span, ch), BF16),
            pltpu.VMEM((2, NCH, nz - 1, span, ch), BF16),
            pltpu.VMEM((2, span, ch), F32),
            pltpu.VMEM((2, NCH, nz, span, ch), BF16),
            pltpu.VMEM((NCH, 2, feats, ch), F32),
            pltpu.VMEM((NCH, 2, ch, feats), F32),
            pltpu.VMEM((2, 2, span, feats), F32),
            pltpu.VMEM((2, nz, 16, t, feats), BF16),
            pltpu.VMEM((2, nz, 15, t, feats), BF16),
            pltpu.VMEM((NCH, 2, feats // 2, ch), BF16),
            pltpu.VMEM((NCH, 2, ch // 2, feats), BF16),
            pltpu.VMEM((NCH, 2, feats // 2, ch), BF16),
            pltpu.VMEM((NCH, 2, ch // 2, feats), BF16),
            pltpu.VMEM((NCH, feats // 2, ch), BF16),
            pltpu.VMEM((NCH, ch // 2, feats), BF16),
            dma((3, NCH)),
            dma((2, 16)),
            dma((2, 16)),
            dma((2, 2, NCH)),
            dma((2, 2, NCH)),
            dma((2, NCH, nz)),
            dma((2, NCH, nz)),
            dma((2, NCH, nz)),
            dma((2, NCH, nz)),
            dma((2, 4, nz)),
            dma((2, 4, nz)),
            dma((4, 2, NCH)),
            dma((4, 2, NCH)),
            dma((2, 2, NCH)),
        ],
        compiler_params=pltpu.CompilerParams(
            collective_id=0, has_side_effects=True, vmem_limit_bytes=62 * 1024 * 1024
        ),
        name="ffn_ring",
    )(x, dy, wu, wd)


def solution(mesh):
    tokens = P(("col", "rep"), "row")
    up, down = P("row", "col"), P("col", "row")
    return jax.shard_map(
        functools.partial(body, mesh.shape["row"], mesh.shape["col"]),
        mesh=mesh,
        in_specs=(tokens, tokens, up, up, down, down),
        out_specs=(tokens, tokens, up, down),
        check_vma=False,
    )
```

```python
import functools

import jax
import jax.numpy as jnp
from jax import lax
from jax.experimental import pallas as pl
from jax.experimental.pallas import tpu as pltpu
from jax.sharding import PartitionSpec as P

MESH = pl.DeviceIdType.MESH
BLOCK = 32
NCH = 3
F32 = jnp.float32
BF16 = jnp.bfloat16
GATHER = (("ya", "yb", "xa", "xb"), ("ya", "xb", "xa", "yb"))
HALVE = (("xa", "xb", "ya", "yb"), ("yb", "ya", "xb", "xa"))


def decode(codes, unit):
    negative = codes >= 127
    size = jnp.where(negative, codes - 127, codes)
    mant = (size & 7) | (jnp.minimum(size, 8) & 8)
    whole = jnp.left_shift(mant, jnp.maximum(jnp.right_shift(size, 3), 1) - 1)
    value = whole.astype(F32) * unit
    return jnp.where(negative, -value, value).astype(BF16)


def units(scales):
    return jnp.left_shift(jnp.ones_like(scales), scales + 15).astype(F32) * (2.0**-24)


def nn(a, b):
    return jnp.dot(a, b, preferred_element_type=F32)


def nt(a, b):
    return lax.dot_general(a, b, (((1,), (1,)), ((), ())), preferred_element_type=F32)


def tn(a, b):
    return lax.dot_general(a, b, (((0,), (0,)), ((), ())), preferred_element_type=F32)


def kernel(
    nz, x_in, dy_in, cu_in, cd_in, su_in, sd_in,
    lo, ig, up_out, down_out,
    tok_v, wu_v, wd_v, rs_rcv, rs_snd, pre_v, ag, ug, dg, acc, obuf, rbuf,
    gs_u, gs_d, gr_u, gr_d, nb_u, nb_d, c_own, c_far, w_snd_v, unit_v,
    loc_sem, c_sem, g_snd, g_rcv, w_snd, w_rcv, rs_ss, rs_rs, ag_ss, ag_rs, p_ss, p_rs, t_snd, t_rcv, t_loc,
):
    t, feats = x_in.shape[1], x_in.shape[2]
    hid = cu_in.shape[1] // 2
    ch = hid // NCH
    fh = feats // 2
    row, col, rep = lax.axis_index("row"), lax.axis_index("col"), lax.axis_index("rep")
    z, yl = row // 2, row % 2
    xx, yh = col // 2, col % 2
    oh, orep = 1 - yl, 1 - rep

    def place(dims):
        a, b = int("ya" in dims), int("yb" in dims)
        nyl, nyh = (yl + a + b) % 2, (yh + b) % 2
        if "xa" in dims and "xb" in dims:
            nx = (xx + 2) % 4
        elif "xa" in dims:
            nx = xx + 1 - 2 * (xx % 2)
        elif "xb" in dims:
            nx = 3 - xx
        else:
            nx = xx
        return nyl, 2 * nx + nyh

    def plane(dim):
        nyl, ncol = place((dim,))
        return (2 * z + nyl, ncol, rep)

    zp = (2 * ((z + 1) % nz) + yl, col, rep)
    zm = (2 * ((z + nz - 1) % nz) + yl, col, rep)
    twin = (row, col, orep)
    ring = (zp, zm)

    def remote(src, dst, ssem, rsem, dev):
        return pltpu.make_async_remote_copy(
            src_ref=src, dst_ref=dst, send_sem=ssem, recv_sem=rsem, device_id=dev, device_id_type=MESH
        )

    def lanes(half, j):
        return pl.ds(pl.multiple_of(half * hid + j * ch, 128), ch)

    def rows(start, size):
        return pl.ds(pl.multiple_of(start, 16), size)

    def code_copy(m, j, far):
        src = (cu_in, cd_in)[m]
        if far:
            return pltpu.make_async_copy(src.at[rows(rep * fh, fh), lanes(oh, j)], c_far.at[m, j], c_sem.at[1, m, j])
        return pltpu.make_async_copy(src.at[:, lanes(yl, j)], c_own.at[m, j], c_sem.at[0, m, j])

    for far in (True, False):
        for j in range(NCH):
            for m in range(2):
                code_copy(m, j, far).start()

    barrier = pltpu.get_barrier_semaphore()
    for dev in (zp, zm, twin, plane("ya"), plane("yb"), plane("xa"), plane("xb")):
        pl.semaphore_signal(barrier, inc=1, device_id=dev, device_id_type=MESH)
    pl.semaphore_wait(barrier, 7)

    def w_first(m, j):
        dst = (wu_v, wd_v)[m].at[j, yl, rows(rep * fh, fh)]
        return remote(w_snd_v.at[m, j], dst, w_snd.at[0, m, j], w_rcv.at[0, m, j], plane("ya"))

    def w_second(m, j):
        ref = (wu_v, wd_v)[m].at[j, oh, rows(rep * fh, fh)]
        return remote(ref, ref, w_snd.at[1, m, j], w_rcv.at[1, m, j], twin)

    def w_decode(m, j, far):
        code_copy(m, j, far).wait()
        count = (fh if far else feats) // BLOCK
        base = rep * (fh // BLOCK) if far else 0
        half = oh if far else yl
        if m == 1:
            groups = sd_in.shape[0]
            lane = lax.broadcasted_iota(jnp.int32, (groups, ch), 1) + half * hid + j * ch
            group = lax.broadcasted_iota(jnp.int32, (groups, ch), 0)
            pick = jnp.where(jnp.right_shift(lane, 5) == group, 1.0, 0.0)
            unit_v[...] = tn(units(sd_in[...]), pick)

        def step(b, carry):
            here = rows(b * BLOCK, BLOCK)
            if m == 0:
                unit = units(su_in[pl.ds(base + b, 1), lanes(half, j)])
            else:
                unit = unit_v[rows((base + b) * BLOCK, BLOCK)]
            if far:
                w_snd_v[m, j, here] = decode(c_far[m, j, here], unit)
            else:
                (wu_v, wd_v)[m][j, yl, here] = decode(c_own[m, j, here], unit)
            return carry

        lax.fori_loop(0, count, step, 0)

    tok_in = (x_in, dy_in)

    def spot(m, code):
        dims = tuple(GATHER[m][k] for k in range(4) if code >> k & 1)
        nyl, ncol = place(dims)
        return tok_v.at[m, nyl, :, rows(ncol * t, t)]

    def g_copy(m, code, step):
        src = tok_in[m] if code == 0 else spot(m, code)
        new = code + 2**step
        return remote(src, spot(m, code), g_snd.at[m, new], g_rcv.at[m, new], plane(GATHER[m][step]))

    def g_wait(m, code):
        here = spot(m, code)
        remote(here, here, g_snd.at[m, code], g_rcv.at[m, code], twin).wait_recv()

    for step in range(1, 4):
        for m in range(2):
            g_copy(m, 0, step).start()
    for m in range(2):
        g_copy(m, 0, 0).start()
    tok_local = [pltpu.make_async_copy(tok_in[m], spot(m, 0), loc_sem.at[2, m]) for m in range(2)]
    for m in range(2):
        tok_local[m].start()

    def w_send(j):
        for m in range(2):
            w_decode(m, j, True)
            w_first(m, j).start()

    def w_relay(j):
        for m in range(2):
            w_first(m, j).wait_recv()
            w_second(m, j).start()

    def clear():
        ug[...] = jnp.zeros_like(ug)
        dg[...] = jnp.zeros_like(dg)
        for m in range(2):
            for j in range(NCH):
                rs_rcv[m, j, 0] = jnp.zeros(rs_rcv.shape[3:], BF16)

    between = {
        2: lambda: w_send(1),
        3: lambda: w_send(2),
        4: lambda: w_decode(0, 0, False),
        5: lambda: w_decode(1, 0, False),
        6: lambda: w_decode(0, 1, False),
        7: lambda: w_decode(1, 1, False),
        8: lambda: w_decode(0, 2, False),
        9: lambda: w_decode(1, 2, False),
        10: clear,
        12: lambda: w_relay(0),
        14: lambda: w_relay(1),
    }
    w_send(0)
    for code in range(1, 16):
        if code in between:
            between[code]()
        for m in range(2):
            g_wait(m, code)
            for step in range(4):
                if 2**step > code:
                    g_copy(m, code, step).start()
    for m in range(2):
        tok_local[m].wait()

    def rs_copy(m, j, s):
        return remote(rs_snd.at[m, j, s], rs_rcv.at[m, j, s + 1], rs_ss.at[m, j, s], rs_rs.at[m, j, s + 1], ring[m])

    def rs_wait(m, j, s):
        here = rs_rcv.at[m, j, s]
        remote(here, here, rs_ss.at[m, j, s], rs_rs.at[m, j, s], twin).wait_recv()

    def term(m, j, b):
        if m == 0:
            return nn(tok_v[0, 0, b], wu_v[j, 0]) + nn(tok_v[0, 1, b], wu_v[j, 1])
        return nn(tok_v[1, 0, b], wd_v[j, 0]) + nn(tok_v[1, 1, b], wd_v[j, 1])

    def rs_step(i, carry):
        s, j = i // NCH, i % NCH

        @pl.when(i == 1)
        def _():
            w_relay(2)

        @pl.when(s == 0)
        def _():
            for m in range(2):
                w_second(m, j).wait_recv()

        for m in range(2):
            b = (z + nz - 1 - s) % nz if m == 0 else (z + 1 + s) % nz
            part = term(m, j, b)

            @pl.when(s > 0)
            def _():
                rs_wait(m, j, s)

            rs_snd[m, j, s] = (part + rs_rcv[m, j, s].astype(F32)).astype(BF16)
            rs_copy(m, j, s).start()
        return carry

    lax.fori_loop(0, NCH * (nz - 1), rs_step, 0)

    def ag_copy(m, j, s):
        return remote(ag.at[m, j, s], ag.at[m, j, s + 1], ag_ss.at[m, j, s], ag_rs.at[m, j, s + 1], ring[m])

    def ag_wait(m, j, s):
        here = ag.at[m, j, s]
        remote(here, here, ag_ss.at[m, j, s], ag_rs.at[m, j, s], twin).wait_recv()

    def gelu_step(j, carry):
        for m in range(2):
            pre_v[m] = term(m, j, z)
        for m in range(2):
            rs_wait(m, j, nz - 1)
        pre = pre_v[0] + rs_rcv[0, j, nz - 1].astype(F32)
        back = pre_v[1] + rs_rcv[1, j, nz - 1].astype(F32)
        cdf = 0.5 * (1.0 + lax.erf(pre * 0.7071067811865476))
        density = jnp.exp(-0.5 * pre * pre) * 0.3989422804014327
        ag[0, j, 0] = (pre * cdf).astype(BF16)
        ag[1, j, 0] = (back * (cdf + pre * density)).astype(BF16)
        for m in range(2):
            ag_copy(m, j, 0).start()
        return carry

    lax.fori_loop(0, NCH, gelu_step, 0)

    widths = (8, 4, 2, 1)
    offs = (0, 8, 12, 14)

    def p_copy(m, k, s):
        w = widths[k]
        return remote(
            obuf.at[m, s, pl.ds(w, w)], rbuf.at[m, s, pl.ds(offs[k], w)],
            p_ss.at[m, k, s], p_rs.at[m, k, s], plane(HALVE[m][k]),
        )

    def p_first(m, s):
        for code in range(16):
            dims = tuple(HALVE[m][k] for k in range(4) if code >> (3 - k) & 1)
            nyl, ncol = place(dims)
            obuf[m, s, code] = acc[m, nyl, rows(ncol * t, t)].astype(BF16)
        p_copy(m, 0, s).start()

    def p_next(m, k, s):
        w = widths[k]
        p_copy(m, k, s).wait_recv()
        both = obuf[m, s, 0:w].astype(F32) + rbuf[m, s, offs[k] : offs[k] + w].astype(F32)
        if k < 3:
            obuf[m, s, 0:w] = both.astype(BF16)
            p_copy(m, k + 1, s).start()
        else:
            b = (z + nz - s) % nz if m == 0 else (z + s) % nz
            (lo, ig)[m][rows(b * t, t)] = both[0].astype(BF16)

    def p_step(s):
        for k in range(3, -1, -1):
            q = s - 1 - k

            @pl.when(jnp.logical_and(q >= 0, q < nz))
            def _():
                for m in range(2):
                    p_next(m, k, q)

    def ag_step(i, carry):
        s, j = i // NCH, i % NCH
        for m in range(2):

            @pl.when(s > 0)
            def _():
                ag_wait(m, j, s)

            @pl.when(jnp.logical_and(s > 0, s < nz - 1))
            def _():
                ag_copy(m, j, s).start()

        @pl.when(j == 0)
        def _():
            acc[...] = jnp.zeros_like(acc)

        for y in range(2):
            acc[0, y] += nt(ag[0, j, s], wd_v[j, y])
            acc[1, y] += nt(ag[1, j, s], wu_v[j, y])

        @pl.when(s % 2 == 1)
        def _():
            a_pair = jnp.concatenate([ag[0, j, s - 1], ag[0, j, s]], axis=0)
            h_pair = jnp.concatenate([ag[1, j, s - 1], ag[1, j, s]], axis=0)
            a0, a1 = (z + nz - s + 1) % nz, (z + nz - s) % nz
            h0, h1 = (z + s - 1) % nz, (z + s) % nz
            for y in range(2):
                dg[j, y] += tn(jnp.concatenate([tok_v[1, y, a0], tok_v[1, y, a1]], axis=0), a_pair)
                ug[j, y] += tn(jnp.concatenate([tok_v[0, y, h0], tok_v[0, y, h1]], axis=0), h_pair)

        @pl.when(j == NCH - 1)
        def _():
            for m in range(2):
                p_first(m, s)
            p_step(s)

        return carry

    lax.fori_loop(0, NCH * nz, ag_step, 0)

    def t_pair(m, j):
        src, dst = ((gs_u, gr_u), (gs_d, gr_d))[m]
        return remote(src.at[j], dst.at[j], t_snd.at[0, m, j], t_rcv.at[0, m, j], twin)

    def grad_half(m, j, y, who):
        return (ug, dg)[m][j, y, rows(who * fh, fh)]

    def home(m, j, half, who):
        return (up_out, down_out)[m].at[rows(who * fh, fh), lanes(half, j)]

    mine = (gr_u, gr_d)
    near = (nb_u, nb_d)

    def t_near(m, j):
        return remote(mine[m].at[j, oh], near[m].at[j], t_snd.at[1, m, j], t_rcv.at[1, m, j], plane("ya"))

    def t_own(m, j):
        return pltpu.make_async_copy(mine[m].at[j, yl], home(m, j, yl, rep), t_loc.at[0, m, j])

    def t_twin(m, j, who):
        return remote(mine[m].at[j, yl], home(m, j, yl, who), t_snd.at[2, m, j], t_rcv.at[2, m, j], twin)

    def t_far(m, j):
        return pltpu.make_async_copy(near[m].at[j], home(m, j, oh, rep), t_loc.at[1, m, j])

    def t_relay(m, j, who):
        return remote(near[m].at[j], home(m, j, oh, who), t_snd.at[3, m, j], t_rcv.at[3, m, j], twin)

    def t_a(j, carry):
        for m in range(2):
            for y in range(2):
                (gs_u, gs_d)[m][j, y] = grad_half(m, j, y, orep).astype(BF16)
            t_pair(m, j).start()
        return carry

    lax.fori_loop(0, NCH, t_a, 0)
    p_step(nz)

    def t_b(j, carry):
        for m in range(2):
            t_pair(m, j).wait_recv()
            for y in range(2):
                mine[m][j, y] = (grad_half(m, j, y, rep) + mine[m][j, y].astype(F32)).astype(BF16)
            t_near(m, j).start()
            t_own(m, j).start()
            t_twin(m, j, rep).start()
        return carry

    lax.fori_loop(0, NCH, t_b, 0)
    for s in range(nz + 1, nz + 4):
        p_step(s)

    def t_c(j, carry):
        for m in range(2):
            t_near(m, j).wait_recv()
            t_far(m, j).start()
            t_relay(m, j, rep).start()
        return carry

    lax.fori_loop(0, NCH, t_c, 0)

    def drain_t(j, carry):
        for m in range(2):
            t_own(m, j).wait()
            t_far(m, j).wait()
            t_twin(m, j, orep).wait_recv()
            t_relay(m, j, orep).wait_recv()
            t_pair(m, j).wait_send()
            t_near(m, j).wait_send()
            t_twin(m, j, rep).wait_send()
            t_relay(m, j, rep).wait_send()
            w_first(m, j).wait_send()
            w_second(m, j).wait_send()
        return carry

    lax.fori_loop(0, NCH, drain_t, 0)

    def drain_ring(i, carry):
        s, j = i // NCH, i % NCH
        for m in range(2):
            rs_copy(m, j, s).wait_send()
            ag_copy(m, j, s).wait_send()
        return carry

    lax.fori_loop(0, NCH * (nz - 1), drain_ring, 0)

    def drain_plane(s, carry):
        for m in range(2):
            for k in range(4):
                p_copy(m, k, s).wait_send()
        return carry

    lax.fori_loop(0, nz, drain_plane, 0)
    for m in range(2):
        for code in range(8):
            for step in range(4):
                if 2**step > code:
                    g_copy(m, code, step).wait_send()


def body(n_row, n_col, activations, out_grad, up_codes, up_scales, down_codes, down_scales):
    nz = n_row // 2
    tok, feats = activations.shape
    t = tok // nz
    hid2 = up_codes.shape[1]
    hid = hid2 // 2
    ch = hid // NCH
    span = n_col * t
    x = activations.reshape(nz, t, feats)
    dy = out_grad.reshape(nz, t, feats)
    hbm = pl.BlockSpec(memory_space=pl.ANY)
    vmem = pl.BlockSpec(memory_space=pltpu.VMEM)
    dma = pltpu.SemaphoreType.DMA
    out, in_grad, up_grad, down_grad = pl.pallas_call(
        functools.partial(kernel, nz),
        out_shape=(
            jax.ShapeDtypeStruct((tok, feats), BF16),
            jax.ShapeDtypeStruct((tok, feats), BF16),
            jax.ShapeDtypeStruct((feats, hid2), BF16),
            jax.ShapeDtypeStruct((feats, hid2), BF16),
        ),
        in_specs=[hbm] * 4 + [vmem] * 2,
        out_specs=(vmem, vmem, hbm, hbm),
        scratch_shapes=[
            pltpu.VMEM((2, 2, nz, span, feats), BF16),
            pltpu.VMEM((NCH, 2, feats, ch), BF16),
            pltpu.VMEM((NCH, 2, feats, ch), BF16),
            pltpu.VMEM((2, NCH, nz, span, ch), BF16),
            pltpu.VMEM((2, NCH, nz - 1, span, ch), BF16),
            pltpu.VMEM((2, span, ch), F32),
            pltpu.VMEM((2, NCH, nz, span, ch), BF16),
            pltpu.VMEM((NCH, 2, feats, ch), F32),
            pltpu.VMEM((NCH, 2, feats, ch), F32),
            pltpu.VMEM((2, 2, span, feats), F32),
            pltpu.VMEM((2, nz, 16, t, feats), BF16),
            pltpu.VMEM((2, nz, 15, t, feats), BF16),
            pltpu.VMEM((NCH, 2, feats // 2, ch), BF16),
            pltpu.VMEM((NCH, 2, feats // 2, ch), BF16),
            pltpu.VMEM((NCH, 2, feats // 2, ch), BF16),
            pltpu.VMEM((NCH, 2, feats // 2, ch), BF16),
            pltpu.VMEM((NCH, feats // 2, ch), BF16),
            pltpu.VMEM((NCH, feats // 2, ch), BF16),
            pltpu.VMEM((2, NCH, feats, ch), jnp.int32),
            pltpu.VMEM((2, NCH, feats // 2, ch), jnp.int32),
            pltpu.VMEM((2, NCH, feats // 2, ch), BF16),
            pltpu.VMEM((feats, ch), F32),
            dma((3, NCH)),
            dma((2, 2, NCH)),
            dma((2, 16)),
            dma((2, 16)),
            dma((2, 2, NCH)),
            dma((2, 2, NCH)),
            dma((2, NCH, nz)),
            dma((2, NCH, nz)),
            dma((2, NCH, nz)),
            dma((2, NCH, nz)),
            dma((2, 4, nz)),
            dma((2, 4, nz)),
            dma((4, 2, NCH)),
            dma((4, 2, NCH)),
            dma((2, 2, NCH)),
        ],
        compiler_params=pltpu.CompilerParams(
            collective_id=0, has_side_effects=True, vmem_limit_bytes=62 * 1024 * 1024
        ),
        name="ffn_ring",
    )(x, dy, up_codes, down_codes.T, up_scales, down_scales)
    return out, in_grad, up_grad, down_grad.T


def solution(mesh):
    tokens = P(("col", "rep"), "row")
    up, down = P("row", "col"), P("col", "row")
    return jax.shard_map(
        functools.partial(body, mesh.shape["row"], mesh.shape["col"]),
        mesh=mesh,
        in_specs=(tokens, tokens, up, up, down, down),
        out_specs=(tokens, tokens, up, down),
        check_vma=False,
    )
```

```python
import functools

import jax
import jax.numpy as jnp
from jax import lax
from jax.experimental import pallas as pl
from jax.experimental.pallas import tpu as pltpu
from jax.sharding import PartitionSpec as P

MESH = pl.DeviceIdType.MESH
BLOCK = 32
NCH = 3
LAG = 1
F32 = jnp.float32
BF16 = jnp.bfloat16
GATHER = (("ya", "yb", "xa", "xb"), ("ya", "xb", "xa", "yb"))
HALVE = (("xa", "xb", "ya", "yb"), ("yb", "ya", "xb", "xa"))


def decode(codes, unit):
    negative = codes >= 127
    size = jnp.where(negative, codes - 127, codes)
    mant = (size & 7) | (jnp.minimum(size, 8) & 8)
    whole = jnp.left_shift(mant, jnp.maximum(jnp.right_shift(size, 3), 1) - 1)
    value = whole.astype(F32) * unit
    return jnp.where(negative, -value, value).astype(BF16)


def units(scales):
    return jnp.left_shift(jnp.ones_like(scales), scales + 15).astype(F32) * (2.0**-24)


def nn(a, b):
    return jnp.dot(a, b, preferred_element_type=F32)


def nt(a, b):
    return lax.dot_general(a, b, (((1,), (1,)), ((), ())), preferred_element_type=F32)


def tn(a, b):
    return lax.dot_general(a, b, (((0,), (0,)), ((), ())), preferred_element_type=F32)


def kernel(
    nz, x_in, dy_in, cu_in, cd_in, su_in, sd_in,
    lo, ig, up_out, down_out,
    tok_v, wu_v, wd_v, rs_rcv, rs_snd, pre_v, ag, ug, dg, acc, obuf, rbuf,
    gs_u, gs_d, gr_u, gr_d, nb_u, nb_d, c_own, c_far, w_snd_v, unit_v,
    loc_sem, c_sem, g_snd, g_rcv, w_snd, w_rcv, rs_ss, rs_rs, ag_ss, ag_rs, p_ss, p_rs, t_snd, t_rcv, t_loc,
):
    t, feats = x_in.shape[1], x_in.shape[2]
    hid = cu_in.shape[1] // 2
    ch = hid // NCH
    fh = feats // 2
    row, col, rep = lax.axis_index("row"), lax.axis_index("col"), lax.axis_index("rep")
    z, yl = row // 2, row % 2
    xx, yh = col // 2, col % 2
    oh, orep = 1 - yl, 1 - rep

    def place(dims):
        a, b = int("ya" in dims), int("yb" in dims)
        nyl, nyh = (yl + a + b) % 2, (yh + b) % 2
        if "xa" in dims and "xb" in dims:
            nx = (xx + 2) % 4
        elif "xa" in dims:
            nx = xx + 1 - 2 * (xx % 2)
        elif "xb" in dims:
            nx = 3 - xx
        else:
            nx = xx
        return nyl, 2 * nx + nyh

    def plane(dim):
        nyl, ncol = place((dim,))
        return (2 * z + nyl, ncol, rep)

    zp = (2 * ((z + 1) % nz) + yl, col, rep)
    zm = (2 * ((z + nz - 1) % nz) + yl, col, rep)
    twin = (row, col, orep)
    ring = (zp, zm)

    def remote(src, dst, ssem, rsem, dev):
        return pltpu.make_async_remote_copy(
            src_ref=src, dst_ref=dst, send_sem=ssem, recv_sem=rsem, device_id=dev, device_id_type=MESH
        )

    def lanes(half, j):
        return pl.ds(pl.multiple_of(half * hid + j * ch, 128), ch)

    def rows(start, size):
        return pl.ds(pl.multiple_of(start, 16), size)

    def code_copy(m, j, far):
        src = (cu_in, cd_in)[m]
        if far:
            return pltpu.make_async_copy(src.at[rows(rep * fh, fh), lanes(oh, j)], c_far.at[m, j], c_sem.at[1, m, j])
        return pltpu.make_async_copy(src.at[:, lanes(yl, j)], c_own.at[m, j], c_sem.at[0, m, j])

    for far in (True, False):
        for j in range(NCH):
            for m in range(2):
                code_copy(m, j, far).start()

    barrier = pltpu.get_barrier_semaphore()
    for dev in (zp, zm, twin, plane("ya"), plane("yb"), plane("xa"), plane("xb")):
        pl.semaphore_signal(barrier, inc=1, device_id=dev, device_id_type=MESH)
    pl.semaphore_wait(barrier, 7)

    def w_first(m, j):
        dst = (wu_v, wd_v)[m].at[j, yl, rows(rep * fh, fh)]
        return remote(w_snd_v.at[m, j], dst, w_snd.at[0, m, j], w_rcv.at[0, m, j], plane("ya"))

    def w_second(m, j):
        ref = (wu_v, wd_v)[m].at[j, oh, rows(rep * fh, fh)]
        return remote(ref, ref, w_snd.at[1, m, j], w_rcv.at[1, m, j], twin)

    def w_decode(m, j, far):
        code_copy(m, j, far).wait()
        count = (fh if far else feats) // BLOCK
        base = rep * (fh // BLOCK) if far else 0
        half = oh if far else yl
        if m == 1:
            groups = sd_in.shape[0]
            lane = lax.broadcasted_iota(jnp.int32, (groups, ch), 1) + half * hid + j * ch
            group = lax.broadcasted_iota(jnp.int32, (groups, ch), 0)
            pick = jnp.where(jnp.right_shift(lane, 5) == group, 1.0, 0.0)
            unit_v[...] = tn(units(sd_in[...]), pick)

        def step(b, carry):
            here = rows(b * BLOCK, BLOCK)
            if m == 0:
                unit = units(su_in[pl.ds(base + b, 1), lanes(half, j)])
            else:
                unit = unit_v[rows((base + b) * BLOCK, BLOCK)]
            if far:
                w_snd_v[m, j, here] = decode(c_far[m, j, here], unit)
            else:
                (wu_v, wd_v)[m][j, yl, here] = decode(c_own[m, j, here], unit)
            return carry

        lax.fori_loop(0, count, step, 0)

    tok_in = (x_in, dy_in)

    def spot(m, code):
        dims = tuple(GATHER[m][k] for k in range(4) if code >> k & 1)
        nyl, ncol = place(dims)
        return tok_v.at[m, nyl, :, rows(ncol * t, t)]

    def g_copy(m, code, step):
        src = tok_in[m] if code == 0 else spot(m, code)
        new = code + 2**step
        return remote(src, spot(m, code), g_snd.at[m, new], g_rcv.at[m, new], plane(GATHER[m][step]))

    def g_wait(m, code):
        here = spot(m, code)
        remote(here, here, g_snd.at[m, code], g_rcv.at[m, code], twin).wait_recv()

    for step in range(1, 4):
        for m in range(2):
            g_copy(m, 0, step).start()
    for m in range(2):
        g_copy(m, 0, 0).start()
    tok_local = [pltpu.make_async_copy(tok_in[m], spot(m, 0), loc_sem.at[2, m]) for m in range(2)]
    for m in range(2):
        tok_local[m].start()

    def w_send(j):
        for m in range(2):
            w_decode(m, j, True)
            w_first(m, j).start()

    def w_relay(j):
        for m in range(2):
            w_first(m, j).wait_recv()
            w_second(m, j).start()

    def clear():
        ug[...] = jnp.zeros_like(ug)
        dg[...] = jnp.zeros_like(dg)
        for m in range(2):
            for j in range(NCH):
                rs_rcv[m, j, 0] = jnp.zeros(rs_rcv.shape[3:], BF16)

    between = {
        2: lambda: w_send(1),
        3: lambda: w_send(2),
        4: lambda: w_decode(0, 0, False),
        5: lambda: w_decode(1, 0, False),
        6: lambda: w_decode(0, 1, False),
        7: lambda: w_decode(1, 1, False),
        8: lambda: w_decode(0, 2, False),
        9: lambda: w_decode(1, 2, False),
        10: clear,
        12: lambda: w_relay(0),
        14: lambda: w_relay(1),
    }
    w_send(0)
    for code in range(1, 16):
        if code in between:
            between[code]()
        for m in range(2):
            g_wait(m, code)
            for step in range(4):
                if 2**step > code:
                    g_copy(m, code, step).start()
    for m in range(2):
        tok_local[m].wait()

    def rs_copy(m, j, s):
        return remote(rs_snd.at[m, j, s], rs_rcv.at[m, j, s + 1], rs_ss.at[m, j, s], rs_rs.at[m, j, s + 1], ring[m])

    def rs_wait(m, j, s):
        here = rs_rcv.at[m, j, s]
        remote(here, here, rs_ss.at[m, j, s], rs_rs.at[m, j, s], twin).wait_recv()

    def term(m, j, b):
        if m == 0:
            return nn(tok_v[0, 0, b], wu_v[j, 0]) + nn(tok_v[0, 1, b], wu_v[j, 1])
        return nn(tok_v[1, 0, b], wd_v[j, 0]) + nn(tok_v[1, 1, b], wd_v[j, 1])

    def rs_step(s, j):
        @pl.when(s == 0)
        def _():
            for m in range(2):
                w_second(m, j).wait_recv()

        for m in range(2):
            b = (z + nz - 1 - s) % nz if m == 0 else (z + 1 + s) % nz
            part = term(m, j, b)

            @pl.when(s > 0)
            def _():
                rs_wait(m, j, s)

            rs_snd[m, j, s] = (part + rs_rcv[m, j, s].astype(F32)).astype(BF16)
            rs_copy(m, j, s).start()

    def ag_copy(m, j, s):
        return remote(ag.at[m, j, s], ag.at[m, j, s + 1], ag_ss.at[m, j, s], ag_rs.at[m, j, s + 1], ring[m])

    def ag_wait(m, j, s):
        here = ag.at[m, j, s]
        remote(here, here, ag_ss.at[m, j, s], ag_rs.at[m, j, s], twin).wait_recv()

    def gelu_step(j):
        for m in range(2):
            pre_v[m] = term(m, j, z)
        for m in range(2):
            rs_wait(m, j, nz - 1)
        pre = pre_v[0] + rs_rcv[0, j, nz - 1].astype(F32)
        back = pre_v[1] + rs_rcv[1, j, nz - 1].astype(F32)
        cdf = 0.5 * (1.0 + lax.erf(pre * 0.7071067811865476))
        density = jnp.exp(-0.5 * pre * pre) * 0.3989422804014327
        ag[0, j, 0] = (pre * cdf).astype(BF16)
        ag[1, j, 0] = (back * (cdf + pre * density)).astype(BF16)
        for m in range(2):
            ag_copy(m, j, 0).start()

    slots = acc.shape[0]
    widths = (8, 4, 2, 1)
    offs = (0, 8, 12, 14)

    def p_copy(m, k, s):
        w = widths[k]
        return remote(
            obuf.at[m, s, pl.ds(w, w)], rbuf.at[m, s, pl.ds(offs[k], w)],
            p_ss.at[m, k, s], p_rs.at[m, k, s], plane(HALVE[m][k]),
        )

    def p_first(m, s):
        for code in range(16):
            dims = tuple(HALVE[m][k] for k in range(4) if code >> (3 - k) & 1)
            nyl, ncol = place(dims)
            obuf[m, s, code] = acc[s % slots, m, nyl, rows(ncol * t, t)].astype(BF16)
        p_copy(m, 0, s).start()

    def p_next(m, k, s):
        w = widths[k]
        p_copy(m, k, s).wait_recv()
        both = obuf[m, s, 0:w].astype(F32) + rbuf[m, s, offs[k] : offs[k] + w].astype(F32)
        if k < 3:
            obuf[m, s, 0:w] = both.astype(BF16)
            p_copy(m, k + 1, s).start()
        else:
            b = (z + nz - s) % nz if m == 0 else (z + s) % nz
            (lo, ig)[m][rows(b * t, t)] = both[0].astype(BF16)

    def p_step(s):
        for k in range(3, -1, -1):
            q = s - 1 - k

            @pl.when(jnp.logical_and(q >= 0, q < nz))
            def _():
                for m in range(2):
                    p_next(m, k, q)

    def ag_step(s, j):
        for m in range(2):

            @pl.when(s > 0)
            def _():
                ag_wait(m, j, s)

            @pl.when(jnp.logical_and(s > 0, s < nz - 1))
            def _():
                ag_copy(m, j, s).start()

        @pl.when(j == 0)
        def _():
            acc[s % slots] = jnp.zeros(acc.shape[1:], F32)

        for y in range(2):
            acc[s % slots, 0, y] += nt(ag[0, j, s], wd_v[j, y])
            acc[s % slots, 1, y] += nt(ag[1, j, s], wu_v[j, y])

        @pl.when(s % 2 == 1)
        def _():
            a_pair = jnp.concatenate([ag[0, j, s - 1], ag[0, j, s]], axis=0)
            h_pair = jnp.concatenate([ag[1, j, s - 1], ag[1, j, s]], axis=0)
            a0, a1 = (z + nz - s + 1) % nz, (z + nz - s) % nz
            h0, h1 = (z + s - 1) % nz, (z + s) % nz
            for y in range(2):
                dg[j, y] += tn(jnp.concatenate([tok_v[1, y, a0], tok_v[1, y, a1]], axis=0), a_pair)
                ug[j, y] += tn(jnp.concatenate([tok_v[0, y, h0], tok_v[0, y, h1]], axis=0), h_pair)

    def t_pair(m, j):
        src, dst = ((gs_u, gr_u), (gs_d, gr_d))[m]
        return remote(src.at[j], dst.at[j], t_snd.at[0, m, j], t_rcv.at[0, m, j], twin)

    def grad_half(m, j, y, who):
        return (ug, dg)[m][j, y, rows(who * fh, fh)]

    def home(m, j, half, who):
        return (up_out, down_out)[m].at[rows(who * fh, fh), lanes(half, j)]

    mine = (gr_u, gr_d)
    near = (nb_u, nb_d)

    def t_near(m, j):
        return remote(mine[m].at[j, oh], near[m].at[j], t_snd.at[1, m, j], t_rcv.at[1, m, j], plane("ya"))

    def t_own(m, j):
        return pltpu.make_async_copy(mine[m].at[j, yl], home(m, j, yl, rep), t_loc.at[0, m, j])

    def t_twin(m, j, who):
        return remote(mine[m].at[j, yl], home(m, j, yl, who), t_snd.at[2, m, j], t_rcv.at[2, m, j], twin)

    def t_far(m, j):
        return pltpu.make_async_copy(near[m].at[j], home(m, j, oh, rep), t_loc.at[1, m, j])

    def t_relay(m, j, who):
        return remote(near[m].at[j], home(m, j, oh, who), t_snd.at[3, m, j], t_rcv.at[3, m, j], twin)

    def t_a(j):
        for m in range(2):
            for y in range(2):
                (gs_u, gs_d)[m][j, y] = grad_half(m, j, y, orep).astype(BF16)
            t_pair(m, j).start()

    def t_b(j):
        for m in range(2):
            t_pair(m, j).wait_recv()
            for y in range(2):
                mine[m][j, y] = (grad_half(m, j, y, rep) + mine[m][j, y].astype(F32)).astype(BF16)
            t_near(m, j).start()
            t_own(m, j).start()
            t_twin(m, j, rep).start()

    def t_c(j):
        for m in range(2):
            t_near(m, j).wait_recv()
            t_far(m, j).start()
            t_relay(m, j, rep).start()

    def ring_step(i, carry):
        j = i % NCH
        q = i // NCH - LAG * j
        s = q - (nz - 1)

        @pl.when(i == 2 * NCH - 1)
        def _():
            w_relay(2)

        @pl.when(jnp.logical_and(q >= 0, q < nz - 1))
        def _():
            rs_step(q, j)

        @pl.when(q == nz - 1)
        def _():
            gelu_step(j)

        @pl.when(jnp.logical_and(s >= 0, s < nz))
        def _():
            ag_step(s, j)

        @pl.when(s == nz - 1)
        def _():
            t_a(j)

        @pl.when(s == nz)
        def _():
            t_b(j)

        @pl.when(s == nz + 2)
        def _():
            t_c(j)

        @pl.when(jnp.logical_and(j == NCH - 1, s >= 0))
        def _():
            @pl.when(s < nz)
            def _():
                for m in range(2):
                    p_first(m, s)

            p_step(s)

        return carry

    lax.fori_loop(0, NCH * (2 * nz + 3 + LAG * (NCH - 1)), ring_step, 0)

    def drain_t(j, carry):
        for m in range(2):
            t_own(m, j).wait()
            t_far(m, j).wait()
            t_twin(m, j, orep).wait_recv()
            t_relay(m, j, orep).wait_recv()
            t_pair(m, j).wait_send()
            t_near(m, j).wait_send()
            t_twin(m, j, rep).wait_send()
            t_relay(m, j, rep).wait_send()
            w_first(m, j).wait_send()
            w_second(m, j).wait_send()
        return carry

    lax.fori_loop(0, NCH, drain_t, 0)

    def drain_ring(i, carry):
        s, j = i // NCH, i % NCH
        for m in range(2):
            rs_copy(m, j, s).wait_send()
            ag_copy(m, j, s).wait_send()
        return carry

    lax.fori_loop(0, NCH * (nz - 1), drain_ring, 0)

    def drain_plane(s, carry):
        for m in range(2):
            for k in range(4):
                p_copy(m, k, s).wait_send()
        return carry

    lax.fori_loop(0, nz, drain_plane, 0)
    for m in range(2):
        for code in range(8):
            for step in range(4):
                if 2**step > code:
                    g_copy(m, code, step).wait_send()


def body(n_row, n_col, activations, out_grad, up_codes, up_scales, down_codes, down_scales):
    nz = n_row // 2
    tok, feats = activations.shape
    t = tok // nz
    hid2 = up_codes.shape[1]
    hid = hid2 // 2
    ch = hid // NCH
    span = n_col * t
    x = activations.reshape(nz, t, feats)
    dy = out_grad.reshape(nz, t, feats)
    hbm = pl.BlockSpec(memory_space=pl.ANY)
    vmem = pl.BlockSpec(memory_space=pltpu.VMEM)
    dma = pltpu.SemaphoreType.DMA
    out, in_grad, up_grad, down_grad = pl.pallas_call(
        functools.partial(kernel, nz),
        out_shape=(
            jax.ShapeDtypeStruct((tok, feats), BF16),
            jax.ShapeDtypeStruct((tok, feats), BF16),
            jax.ShapeDtypeStruct((feats, hid2), BF16),
            jax.ShapeDtypeStruct((feats, hid2), BF16),
        ),
        in_specs=[hbm] * 4 + [vmem] * 2,
        out_specs=(vmem, vmem, hbm, hbm),
        scratch_shapes=[
            pltpu.VMEM((2, 2, nz, span, feats), BF16),
            pltpu.VMEM((NCH, 2, feats, ch), BF16),
            pltpu.VMEM((NCH, 2, feats, ch), BF16),
            pltpu.VMEM((2, NCH, nz, span, ch), BF16),
            pltpu.VMEM((2, NCH, nz - 1, span, ch), BF16),
            pltpu.VMEM((2, span, ch), F32),
            pltpu.VMEM((2, NCH, nz, span, ch), BF16),
            pltpu.VMEM((NCH, 2, feats, ch), F32),
            pltpu.VMEM((NCH, 2, feats, ch), F32),
            pltpu.VMEM((LAG * (NCH - 1) + 1, 2, 2, span, feats), F32),
            pltpu.VMEM((2, nz, 16, t, feats), BF16),
            pltpu.VMEM((2, nz, 15, t, feats), BF16),
            pltpu.VMEM((NCH, 2, feats // 2, ch), BF16),
            pltpu.VMEM((NCH, 2, feats // 2, ch), BF16),
            pltpu.VMEM((NCH, 2, feats // 2, ch), BF16),
            pltpu.VMEM((NCH, 2, feats // 2, ch), BF16),
            pltpu.VMEM((NCH, feats // 2, ch), BF16),
            pltpu.VMEM((NCH, feats // 2, ch), BF16),
            pltpu.VMEM((2, NCH, feats, ch), jnp.int32),
            pltpu.VMEM((2, NCH, feats // 2, ch), jnp.int32),
            pltpu.VMEM((2, NCH, feats // 2, ch), BF16),
            pltpu.VMEM((feats, ch), F32),
            dma((3, NCH)),
            dma((2, 2, NCH)),
            dma((2, 16)),
            dma((2, 16)),
            dma((2, 2, NCH)),
            dma((2, 2, NCH)),
            dma((2, NCH, nz)),
            dma((2, NCH, nz)),
            dma((2, NCH, nz)),
            dma((2, NCH, nz)),
            dma((2, 4, nz)),
            dma((2, 4, nz)),
            dma((4, 2, NCH)),
            dma((4, 2, NCH)),
            dma((2, 2, NCH)),
        ],
        compiler_params=pltpu.CompilerParams(
            collective_id=0, has_side_effects=True, vmem_limit_bytes=62 * 1024 * 1024
        ),
        name="ffn_ring",
    )(x, dy, up_codes, down_codes.T, up_scales, down_scales)
    return out, in_grad, up_grad, down_grad.T


def solution(mesh):
    tokens = P(("col", "rep"), "row")
    up, down = P("row", "col"), P("col", "row")
    return jax.shard_map(
        functools.partial(body, mesh.shape["row"], mesh.shape["col"]),
        mesh=mesh,
        in_specs=(tokens, tokens, up, up, down, down),
        out_specs=(tokens, tokens, up, down),
        check_vma=False,
    )
```

```python
import functools

import jax
import jax.numpy as jnp
from jax import lax
from jax.experimental import pallas as pl
from jax.experimental.pallas import tpu as pltpu
from jax.sharding import PartitionSpec as P

MESH = pl.DeviceIdType.MESH
BLOCK = 32
NCH = 3
LAG = 1
F32 = jnp.float32
BF16 = jnp.bfloat16
GATHER = (("ya", "yb", "xa", "xb"), ("ya", "xb", "xa", "yb"))
HALVE = (("xa", "xb", "ya", "yb"), ("yb", "ya", "xb", "xa"))


def decode(codes, unit):
    negative = codes >= 127
    size = jnp.where(negative, codes - 127, codes)
    mant = (size & 7) | (jnp.minimum(size, 8) & 8)
    whole = jnp.left_shift(mant, jnp.maximum(jnp.right_shift(size, 3), 1) - 1)
    value = whole.astype(F32) * unit
    return jnp.where(negative, -value, value).astype(BF16)


def units(scales):
    return jnp.left_shift(jnp.ones_like(scales), scales + 15).astype(F32) * (2.0**-24)


def nn(a, b):
    return jnp.dot(a, b, preferred_element_type=F32)


def nt(a, b):
    return lax.dot_general(a, b, (((1,), (1,)), ((), ())), preferred_element_type=F32)


def tn(a, b):
    return lax.dot_general(a, b, (((0,), (0,)), ((), ())), preferred_element_type=F32)


def kernel(
    nz, x_in, dy_in, cu_in, cd_in, su_in, sd_in,
    lo, ig, up_out, down_out,
    tok_v, wu_v, wd_v, rs_rcv, rs_snd, pre_v, ag, ug, dg, acc, obuf, rbuf,
    gs_u, gs_d, gr_u, gr_d, nb_u, nb_d, c_own, c_far, w_snd_v, unit_v,
    loc_sem, c_sem, g_snd, g_rcv, w_snd, w_rcv, rs_ss, rs_rs, ag_ss, ag_rs, p_ss, p_rs, t_snd, t_rcv, t_loc,
):
    t, feats = x_in.shape[1], x_in.shape[2]
    hid = cu_in.shape[1] // 2
    ch = hid // NCH
    fh = feats // 2
    row, col, rep = lax.axis_index("row"), lax.axis_index("col"), lax.axis_index("rep")
    z, yl = row // 2, row % 2
    xx, yh = col // 2, col % 2
    oh, orep = 1 - yl, 1 - rep

    def place(dims):
        a, b = int("ya" in dims), int("yb" in dims)
        nyl, nyh = (yl + a + b) % 2, (yh + b) % 2
        if "xa" in dims and "xb" in dims:
            nx = (xx + 2) % 4
        elif "xa" in dims:
            nx = xx + 1 - 2 * (xx % 2)
        elif "xb" in dims:
            nx = 3 - xx
        else:
            nx = xx
        return nyl, 2 * nx + nyh

    def plane(dim):
        nyl, ncol = place((dim,))
        return (2 * z + nyl, ncol, rep)

    zp = (2 * ((z + 1) % nz) + yl, col, rep)
    zm = (2 * ((z + nz - 1) % nz) + yl, col, rep)
    twin = (row, col, orep)
    ring = (zp, zm)

    def remote(src, dst, ssem, rsem, dev):
        return pltpu.make_async_remote_copy(
            src_ref=src, dst_ref=dst, send_sem=ssem, recv_sem=rsem, device_id=dev, device_id_type=MESH
        )

    def lanes(half, j):
        return pl.ds(pl.multiple_of(half * hid + j * ch, 128), ch)

    def rows(start, size):
        return pl.ds(pl.multiple_of(start, 16), size)

    def code_copy(m, j, far):
        src = (cu_in, cd_in)[m]
        if far:
            return pltpu.make_async_copy(src.at[rows(rep * fh, fh), lanes(oh, j)], c_far.at[m, j], c_sem.at[1, m, j])
        return pltpu.make_async_copy(src.at[:, lanes(yl, j)], c_own.at[m, j], c_sem.at[0, m, j])

    tok_in = (x_in, dy_in)

    def tok_local(m, k):
        b = (z + nz - 1 - k) % nz if m == 0 else (z + 1 + k) % nz
        return pltpu.make_async_copy(tok_in[m].at[b], tok_v.at[m, yl, k, rows(col * t, t)], loc_sem.at[m, k])

    for k in range(nz):
        for m in range(2):
            tok_local(m, k).start()
    for far in (True, False):
        for j in range(NCH):
            for m in range(2):
                code_copy(m, j, far).start()

    barrier = pltpu.get_barrier_semaphore()
    for dev in (zp, zm, twin, plane("ya"), plane("yb"), plane("xa"), plane("xb")):
        pl.semaphore_signal(barrier, inc=1, device_id=dev, device_id_type=MESH)
    pl.semaphore_wait(barrier, 7)

    def w_first(m, j):
        dst = (wu_v, wd_v)[m].at[j, yl, rows(rep * fh, fh)]
        return remote(w_snd_v.at[m, j], dst, w_snd.at[0, m, j], w_rcv.at[0, m, j], plane("ya"))

    def w_second(m, j):
        ref = (wu_v, wd_v)[m].at[j, oh, rows(rep * fh, fh)]
        return remote(ref, ref, w_snd.at[1, m, j], w_rcv.at[1, m, j], twin)

    def w_decode(m, j, far):
        code_copy(m, j, far).wait()
        count = (fh if far else feats) // BLOCK
        base = rep * (fh // BLOCK) if far else 0
        half = oh if far else yl
        if m == 1:
            groups = sd_in.shape[0]
            lane = lax.broadcasted_iota(jnp.int32, (groups, ch), 1) + half * hid + j * ch
            group = lax.broadcasted_iota(jnp.int32, (groups, ch), 0)
            pick = jnp.where(jnp.right_shift(lane, 5) == group, 1.0, 0.0)
            unit_v[...] = tn(units(sd_in[...]), pick)

        def step(b, carry):
            here = rows(b * BLOCK, BLOCK)
            if m == 0:
                unit = units(su_in[pl.ds(base + b, 1), lanes(half, j)])
            else:
                unit = unit_v[rows((base + b) * BLOCK, BLOCK)]
            if far:
                w_snd_v[m, j, here] = decode(c_far[m, j, here], unit)
            else:
                (wu_v, wd_v)[m][j, yl, here] = decode(c_own[m, j, here], unit)
            return carry

        lax.fori_loop(0, count, step, 0)

    gz = nz // 2

    def spot(m, code, g):
        dims = tuple(GATHER[m][k] for k in range(4) if code >> k & 1)
        nyl, ncol = place(dims)
        return tok_v.at[m, nyl, pl.ds(g * gz, gz), rows(ncol * t, t)]

    def g_copy(m, code, step, g):
        new = code + 2**step
        here = spot(m, code, g)
        return remote(here, here, g_snd.at[m, new, g], g_rcv.at[m, new, g], plane(GATHER[m][step]))

    def g_pass(code, g):
        for m in range(2):
            here = spot(m, code, g)
            remote(here, here, g_snd.at[m, code, g], g_rcv.at[m, code, g], twin).wait_recv()
            for step in range(4):
                if 2**step > code:
                    g_copy(m, code, step, g).start()

    for g in range(2):
        for k in range(g * gz, g * gz + gz):
            for m in range(2):
                tok_local(m, k).wait()
        for step in (3, 2, 1, 0) if g == 0 else (0,):
            for m in range(2):
                g_copy(m, 0, step, g).start()

    def w_send(j):
        for m in range(2):
            w_decode(m, j, True)
            w_first(m, j).start()

    def w_relay(j):
        for m in range(2):
            w_first(m, j).wait_recv()
            w_second(m, j).start()

    def clear():
        ug[...] = jnp.zeros_like(ug)
        dg[...] = jnp.zeros_like(dg)
        for m in range(2):
            for j in range(NCH):
                rs_rcv[m, j, 0] = jnp.zeros(rs_rcv.shape[3:], BF16)

    between = {
        2: lambda: w_send(1),
        3: lambda: w_send(2),
        4: lambda: w_decode(0, 0, False),
        5: lambda: w_decode(1, 0, False),
        6: lambda: w_decode(0, 1, False),
        7: lambda: w_decode(1, 1, False),
        9: lambda: w_decode(0, 2, False),
        10: lambda: w_decode(1, 2, False),
        11: clear,
        13: lambda: w_relay(0),
    }
    w_send(0)
    for code in range(1, 16):
        if code in between:
            between[code]()
        g_pass(code, 0)
        if code == 7:
            for step in (3, 2, 1):
                for m in range(2):
                    g_copy(m, 0, step, 1).start()

    def rs_copy(m, j, s):
        return remote(rs_snd.at[m, j, s], rs_rcv.at[m, j, s + 1], rs_ss.at[m, j, s], rs_rs.at[m, j, s + 1], ring[m])

    def rs_wait(m, j, s):
        here = rs_rcv.at[m, j, s]
        remote(here, here, rs_ss.at[m, j, s], rs_rs.at[m, j, s], twin).wait_recv()

    def term(m, j, b):
        if m == 0:
            return nn(tok_v[0, 0, b], wu_v[j, 0]) + nn(tok_v[0, 1, b], wu_v[j, 1])
        return nn(tok_v[1, 0, b], wd_v[j, 0]) + nn(tok_v[1, 1, b], wd_v[j, 1])

    def rs_step(s, j):
        @pl.when(s == 0)
        def _():
            for m in range(2):
                w_second(m, j).wait_recv()

        for m in range(2):
            part = term(m, j, s)

            @pl.when(s > 0)
            def _():
                rs_wait(m, j, s)

            rs_snd[m, j, s] = (part + rs_rcv[m, j, s].astype(F32)).astype(BF16)
            rs_copy(m, j, s).start()

    def ag_copy(m, j, s):
        return remote(ag.at[m, j, s], ag.at[m, j, s + 1], ag_ss.at[m, j, s], ag_rs.at[m, j, s + 1], ring[m])

    def ag_wait(m, j, s):
        here = ag.at[m, j, s]
        remote(here, here, ag_ss.at[m, j, s], ag_rs.at[m, j, s], twin).wait_recv()

    def gelu_step(j):
        for m in range(2):
            pre_v[m] = term(m, j, nz - 1)
        for m in range(2):
            rs_wait(m, j, nz - 1)
        pre = pre_v[0] + rs_rcv[0, j, nz - 1].astype(F32)
        back = pre_v[1] + rs_rcv[1, j, nz - 1].astype(F32)
        cdf = 0.5 * (1.0 + lax.erf(pre * 0.7071067811865476))
        density = jnp.exp(-0.5 * pre * pre) * 0.3989422804014327
        ag[0, j, 0] = (pre * cdf).astype(BF16)
        ag[1, j, 0] = (back * (cdf + pre * density)).astype(BF16)
        for m in range(2):
            ag_copy(m, j, 0).start()

    slots = acc.shape[0]
    widths = (8, 4, 2, 1)
    offs = (0, 8, 12, 14)

    def p_copy(m, k, s):
        w = widths[k]
        return remote(
            obuf.at[m, s, pl.ds(w, w)], rbuf.at[m, s, pl.ds(offs[k], w)],
            p_ss.at[m, k, s], p_rs.at[m, k, s], plane(HALVE[m][k]),
        )

    def p_first(m, s):
        for code in range(16):
            dims = tuple(HALVE[m][k] for k in range(4) if code >> (3 - k) & 1)
            nyl, ncol = place(dims)
            obuf[m, s, code] = acc[s % slots, m, nyl, rows(ncol * t, t)].astype(BF16)
        p_copy(m, 0, s).start()

    def p_next(m, k, s):
        w = widths[k]
        p_copy(m, k, s).wait_recv()
        both = obuf[m, s, 0:w].astype(F32) + rbuf[m, s, offs[k] : offs[k] + w].astype(F32)
        if k < 3:
            obuf[m, s, 0:w] = both.astype(BF16)
            p_copy(m, k + 1, s).start()
        else:
            b = (z + nz - s) % nz if m == 0 else (z + s) % nz
            (lo, ig)[m][rows(b * t, t)] = both[0].astype(BF16)

    def p_step(s):
        for k in range(3, -1, -1):
            q = s - 1 - k

            @pl.when(jnp.logical_and(q >= 0, q < nz))
            def _():
                for m in range(2):
                    p_next(m, k, q)

    def ag_step(s, j):
        for m in range(2):

            @pl.when(s > 0)
            def _():
                ag_wait(m, j, s)

            @pl.when(jnp.logical_and(s > 0, s < nz - 1))
            def _():
                ag_copy(m, j, s).start()

        @pl.when(j == 0)
        def _():
            acc[s % slots] = jnp.zeros(acc.shape[1:], F32)

        for y in range(2):
            acc[s % slots, 0, y] += nt(ag[0, j, s], wd_v[j, y])
            acc[s % slots, 1, y] += nt(ag[1, j, s], wu_v[j, y])

        @pl.when(s % 2 == 1)
        def _():
            a_pair = jnp.concatenate([ag[0, j, s - 1], ag[0, j, s]], axis=0)
            h_pair = jnp.concatenate([ag[1, j, s - 1], ag[1, j, s]], axis=0)
            k0, k1 = nz - s, nz - 1 - s
            for y in range(2):
                dg[j, y] += tn(jnp.concatenate([tok_v[1, y, k0], tok_v[1, y, k1]], axis=0), a_pair)
                ug[j, y] += tn(jnp.concatenate([tok_v[0, y, k0], tok_v[0, y, k1]], axis=0), h_pair)

    def t_pair(m, j):
        src, dst = ((gs_u, gr_u), (gs_d, gr_d))[m]
        return remote(src.at[j], dst.at[j], t_snd.at[0, m, j], t_rcv.at[0, m, j], twin)

    def grad_half(m, j, y, who):
        return (ug, dg)[m][j, y, rows(who * fh, fh)]

    def home(m, j, half, who):
        return (up_out, down_out)[m].at[rows(who * fh, fh), lanes(half, j)]

    mine = (gr_u, gr_d)
    near = (nb_u, nb_d)

    def t_near(m, j):
        return remote(mine[m].at[j, oh], near[m].at[j], t_snd.at[1, m, j], t_rcv.at[1, m, j], plane("ya"))

    def t_own(m, j):
        return pltpu.make_async_copy(mine[m].at[j, yl], home(m, j, yl, rep), t_loc.at[0, m, j])

    def t_twin(m, j, who):
        return remote(mine[m].at[j, yl], home(m, j, yl, who), t_snd.at[2, m, j], t_rcv.at[2, m, j], twin)

    def t_far(m, j):
        return pltpu.make_async_copy(near[m].at[j], home(m, j, oh, rep), t_loc.at[1, m, j])

    def t_relay(m, j, who):
        return remote(near[m].at[j], home(m, j, oh, who), t_snd.at[3, m, j], t_rcv.at[3, m, j], twin)

    def t_a(j):
        for m in range(2):
            for y in range(2):
                (gs_u, gs_d)[m][j, y] = grad_half(m, j, y, orep).astype(BF16)
            t_pair(m, j).start()

    def t_b(j):
        for m in range(2):
            t_pair(m, j).wait_recv()
            for y in range(2):
                mine[m][j, y] = (grad_half(m, j, y, rep) + mine[m][j, y].astype(F32)).astype(BF16)
            t_near(m, j).start()
            t_own(m, j).start()
            t_twin(m, j, rep).start()

    def t_c(j):
        for m in range(2):
            t_near(m, j).wait_recv()
            t_far(m, j).start()
            t_relay(m, j, rep).start()

    def ring_step(i, carry):
        j = i % NCH
        q = i // NCH - LAG * j
        s = q - (nz - 1)

        last = gz * NCH - 1
        for k in range(last + 1):

            @pl.when(i == k)
            def _():
                for code in (k + 1,) if k < last else range(k + 1, 16):
                    g_pass(code, 1)

        for k in range(1, NCH):

            @pl.when(i == k * NCH - 1)
            def _():
                w_relay(k)

        @pl.when(jnp.logical_and(q >= 0, q < nz - 1))
        def _():
            rs_step(q, j)

        @pl.when(q == nz - 1)
        def _():
            gelu_step(j)

        @pl.when(jnp.logical_and(s >= 0, s < nz))
        def _():
            ag_step(s, j)

        @pl.when(s == nz - 1)
        def _():
            t_a(j)

        @pl.when(s == nz)
        def _():
            t_b(j)

        @pl.when(s == nz + 2)
        def _():
            t_c(j)

        @pl.when(jnp.logical_and(j == NCH - 1, s >= 0))
        def _():
            @pl.when(s < nz)
            def _():
                for m in range(2):
                    p_first(m, s)

            p_step(s)

        return carry

    lax.fori_loop(0, NCH * (2 * nz + 3 + LAG * (NCH - 1)), ring_step, 0)

    def drain_t(j, carry):
        for m in range(2):
            t_own(m, j).wait()
            t_far(m, j).wait()
            t_twin(m, j, orep).wait_recv()
            t_relay(m, j, orep).wait_recv()
            t_pair(m, j).wait_send()
            t_near(m, j).wait_send()
            t_twin(m, j, rep).wait_send()
            t_relay(m, j, rep).wait_send()
            w_first(m, j).wait_send()
            w_second(m, j).wait_send()
        return carry

    lax.fori_loop(0, NCH, drain_t, 0)

    def drain_ring(i, carry):
        s, j = i // NCH, i % NCH
        for m in range(2):
            rs_copy(m, j, s).wait_send()
            ag_copy(m, j, s).wait_send()
        return carry

    lax.fori_loop(0, NCH * (nz - 1), drain_ring, 0)

    def drain_plane(s, carry):
        for m in range(2):
            for k in range(4):
                p_copy(m, k, s).wait_send()
        return carry

    lax.fori_loop(0, nz, drain_plane, 0)
    for m in range(2):
        for code in range(8):
            for step in range(4):
                if 2**step > code:
                    for g in range(2):
                        g_copy(m, code, step, g).wait_send()


def body(n_row, n_col, activations, out_grad, up_codes, up_scales, down_codes, down_scales):
    nz = n_row // 2
    tok, feats = activations.shape
    t = tok // nz
    hid2 = up_codes.shape[1]
    hid = hid2 // 2
    ch = hid // NCH
    span = n_col * t
    x = activations.reshape(nz, t, feats)
    dy = out_grad.reshape(nz, t, feats)
    hbm = pl.BlockSpec(memory_space=pl.ANY)
    vmem = pl.BlockSpec(memory_space=pltpu.VMEM)
    dma = pltpu.SemaphoreType.DMA
    out, in_grad, up_grad, down_grad = pl.pallas_call(
        functools.partial(kernel, nz),
        out_shape=(
            jax.ShapeDtypeStruct((tok, feats), BF16),
            jax.ShapeDtypeStruct((tok, feats), BF16),
            jax.ShapeDtypeStruct((feats, hid2), BF16),
            jax.ShapeDtypeStruct((feats, hid2), BF16),
        ),
        in_specs=[hbm] * 4 + [vmem] * 2,
        out_specs=(vmem, vmem, hbm, hbm),
        scratch_shapes=[
            pltpu.VMEM((2, 2, nz, span, feats), BF16),
            pltpu.VMEM((NCH, 2, feats, ch), BF16),
            pltpu.VMEM((NCH, 2, feats, ch), BF16),
            pltpu.VMEM((2, NCH, nz, span, ch), BF16),
            pltpu.VMEM((2, NCH, nz - 1, span, ch), BF16),
            pltpu.VMEM((2, span, ch), F32),
            pltpu.VMEM((2, NCH, nz, span, ch), BF16),
            pltpu.VMEM((NCH, 2, feats, ch), F32),
            pltpu.VMEM((NCH, 2, feats, ch), F32),
            pltpu.VMEM((LAG * (NCH - 1) + 1, 2, 2, span, feats), F32),
            pltpu.VMEM((2, nz, 16, t, feats), BF16),
            pltpu.VMEM((2, nz, 15, t, feats), BF16),
            pltpu.VMEM((NCH, 2, feats // 2, ch), BF16),
            pltpu.VMEM((NCH, 2, feats // 2, ch), BF16),
            pltpu.VMEM((NCH, 2, feats // 2, ch), BF16),
            pltpu.VMEM((NCH, 2, feats // 2, ch), BF16),
            pltpu.VMEM((NCH, feats // 2, ch), BF16),
            pltpu.VMEM((NCH, feats // 2, ch), BF16),
            pltpu.VMEM((2, NCH, feats, ch), jnp.int32),
            pltpu.VMEM((2, NCH, feats // 2, ch), jnp.int32),
            pltpu.VMEM((2, NCH, feats // 2, ch), BF16),
            pltpu.VMEM((feats, ch), F32),
            dma((2, nz)),
            dma((2, 2, NCH)),
            dma((2, 16, 2)),
            dma((2, 16, 2)),
            dma((2, 2, NCH)),
            dma((2, 2, NCH)),
            dma((2, NCH, nz)),
            dma((2, NCH, nz)),
            dma((2, NCH, nz)),
            dma((2, NCH, nz)),
            dma((2, 4, nz)),
            dma((2, 4, nz)),
            dma((4, 2, NCH)),
            dma((4, 2, NCH)),
            dma((2, 2, NCH)),
        ],
        compiler_params=pltpu.CompilerParams(
            collective_id=0, has_side_effects=True, vmem_limit_bytes=62 * 1024 * 1024
        ),
        name="ffn_ring",
    )(x, dy, up_codes, down_codes.T, up_scales, down_scales)
    return out, in_grad, up_grad, down_grad.T


def solution(mesh):
    tokens = P(("col", "rep"), "row")
    up, down = P("row", "col"), P("col", "row")
    return jax.shard_map(
        functools.partial(body, mesh.shape["row"], mesh.shape["col"]),
        mesh=mesh,
        in_specs=(tokens, tokens, up, up, down, down),
        out_specs=(tokens, tokens, up, down),
        check_vma=False,
    )
```
